32 devices in a mesh: groups: 2 (over y), tgt: 4 (over z), src: 2 (over x), sub: 2 (over core).
Axes of the slice: x: 2, y: 2, z: 4, core: 2. Of those that a mesh axis runs over, the one named last changes fastest.
Arguments:
- points: float32 [3, 4096], P(None, ('groups', 'tgt', 'src', 'sub')), parts along dimension 1, may hold values from -1.4 to 1.4, as said below
- density: float32 [32, 4096], P(None, ('groups', 'tgt', 'src', 'sub')), parts along dimension 1, may hold values from 0.2 to 2
- incident: float32 [32, 4096], P(None, ('groups', 'tgt', 'src', 'sub')), parts along dimension 1, may hold values from -0.21 to 0.21
- precond: float32 [4096], P(('groups', 'tgt', 'src', 'sub')), parts along dimension 0, may hold values from 0.054414064 to 0.16324219
- receivers: int32 [4096], P('groups'), parts along dimension 0, may hold values from 0 to 65535
Outputs:
- density_out: float32 [32, 4096], P(None, ('groups', 'tgt', 'src', 'sub')), parts along dimension 1
- far_field: float32 [32, 4096], P(None, ('groups', 'tgt', 'src', 'sub')), parts along dimension 1
The draws below stay inside these ranges and needn't reach their ends.
There are 2 independent parts, one for each index of `groups`. The reference program is written for one: setup_inputs(seed, part) draws one part's arguments, and reference() takes and returns one part's arrays. A program takes and returns all parts, laid end to end along the dimension named above; each array names one. Nothing has to cross between parts.
Inputs may be any that keep to these rules, and one draw needn't show every extreme that they name: Coordinates of points of a closed star-shaped surface around the anchor. `receivers`: numbers of directions in the receiver table.
All inputs are finite; a program needn't handle non-finite values.
Results may differ from the reference program's by a relative error of at most 0.0015.
Values may be sent and summed in bfloat16 or wider, within the bound.
A program may use at most 64 MiB of HBM per device.

```python
import math
import jax
import jax.numpy as jnp
from jax import lax

C = 32
PTS_DEV = 128
ITERS = 4
NDIR = 65536
NPTS = 2048
NRCV = 2048


def draw_points(key, part):
    shift_key, phase_key = jax.random.split(jax.random.fold_in(key, 17), 2)
    position = jnp.arange(NPTS)
    patches = NPTS // PTS_DEV
    patch = (position // PTS_DEV).astype(jnp.float32)
    height = 1.0 - (2.0 * patch + 1.0) / patches
    radial = jnp.sqrt(jnp.maximum(1.0 - height * height, 0.0))
    azimuth = patch * 2.399963
    center = jnp.stack([radial * jnp.cos(azimuth), radial * jnp.sin(azimuth), height])
    spread = min(1.6 / math.sqrt(patches), 0.15)
    offsets = jax.random.truncated_normal(shift_key, -3.0, 3.0, (3, NPTS), jnp.float32) * spread
    moved = center + offsets
    unit = moved / jnp.sqrt(jnp.sum(moved * moved, axis=0, keepdims=True))
    phases = jax.random.uniform(phase_key, (3,), jnp.float32, 0.0, 6.283)
    amplitude = 0.12
    radius = 1.0 + amplitude * jnp.sin(3.0 * unit[0] + phases[0]) * jnp.cos(2.0 * unit[1] + phases[1])
    radius = radius + 0.5 * amplitude * jnp.sin(4.0 * unit[2] + phases[2])
    return (unit * radius[None, :]).astype(jnp.float32)


def touch_ends(drawn, key, least, largest):
    longest = drawn.shape.index(max(drawn.shape))
    spots = []
    for shift in (0, 1):
        where = [jax.random.randint(jax.random.fold_in(key, axis), (), 0, length) for axis, length in enumerate(drawn.shape)]
        where[longest] = (where[longest] + shift) % drawn.shape[longest]
        spots.append(tuple(where))
    return drawn.at[spots[0]].set(least).at[spots[1]].set(largest)


def level_of(rng, dims, shards, low, top_value):
    gain, own = 1.0, jax.random.fold_in(rng, 6)
    for dim, shards_of in shards:
        steps = jnp.exp(jax.random.uniform(jax.random.fold_in(own, dim), (shards_of,), jnp.float32, low / len(shards), top_value / len(shards)))
        gain = gain * jnp.repeat(steps, dims[dim] // shards_of).reshape([-1 if axis == dim else 1 for axis in range(len(dims))])
    return gain


def noise(rng, shape, width, limit, cuts=(), held_as=jnp.bfloat16):
    entries = width * jax.random.normal(rng, shape, jnp.float32)
    if cuts:
        entries = entries * level_of(rng, shape, cuts, -0.22, 0.18)
    return jnp.clip(entries, -limit, limit).astype(held_as)


def setup_inputs(seed: int = 0, part: int = 0) -> dict:
    arg_keys = jax.random.split(jax.random.key(seed), 6)
    own_keys = jax.random.split(jax.random.fold_in(arg_keys[5], part), 6)
    return {
        "points": draw_points(jax.random.fold_in(jax.random.fold_in(arg_keys[5], part), 71), part),
        "density": jnp.clip(0.2 + 1.8 * jax.random.uniform(own_keys[1], (C, NPTS), jnp.float32) ** level_of(own_keys[1], (C, NPTS), ((1, 16),), -0.2, 0.2), 0.2, 2.0),
        "incident": noise(own_keys[2], (C, NPTS), 0.035, 0.21, ((1, 16),), jnp.float32),
        "precond": jnp.clip(jnp.exp(math.log(0.16324219) - 1.0986123 * jax.random.uniform(own_keys[3], (NPTS,), jnp.float32) ** level_of(own_keys[3], (NPTS,), ((0, 16),), -0.2, 0.2)), 0.054414064, 0.16324219),
        "receivers": touch_ends(jax.random.randint(own_keys[4], (NRCV,), 0, NDIR), jax.random.fold_in(own_keys[4], 1), 0, NDIR - 1).astype(jnp.int32),
    }


WAVENUMBER = 32.0
SMOOTHING = 0.02
FOUR_PI = 4.0 * math.pi

def single_layer(targets, sources):
    delta_x = targets[0][:, None] - sources[0][None, :]
    delta_y = targets[1][:, None] - sources[1][None, :]
    delta_z = targets[2][:, None] - sources[2][None, :]
    squared = delta_x * delta_x + delta_y * delta_y + delta_z * delta_z
    values = jnp.cos(WAVENUMBER * jnp.sqrt(squared)) / (FOUR_PI * jnp.sqrt(squared + SMOOTHING * SMOOTHING))
    return values.astype(jnp.bfloat16)

def far_kernel(toward, sources):
    projection = toward[0][:, None] * sources[0][None, :] + toward[1][:, None] * sources[1][None, :]
    projection = projection + toward[2][:, None] * sources[2][None, :]
    return jnp.cos(WAVENUMBER * projection).astype(jnp.bfloat16)

def receiver_directions(direction_index):
    upper_part = direction_index // 256
    lower_part = direction_index % 256
    rotation = (upper_part * 14080 + lower_part * 40503) % 65536
    azimuth = rotation.astype(jnp.float32) * (2.0 * math.pi / 65536.0)
    height = 1.0 - (2 * direction_index + 1).astype(jnp.float32) / NDIR
    radial = jnp.sqrt(jnp.maximum(1.0 - height * height, 0.0))
    return jnp.stack([radial * jnp.cos(azimuth), radial * jnp.sin(azimuth), height])

def contract(weighted, kernel_table):
    return lax.dot_general(weighted, kernel_table, (((1,), (1,)), ((), ())), preferred_element_type=jnp.float32)

def blocked(weighted, targets, sources, maker):
    target_count = targets.shape[1]
    block_width = math.gcd(target_count, 1024)
    target_blocks = targets.reshape(3, target_count // block_width, block_width).transpose(1, 0, 2)

    def one_block(target_rows):
        return contract(weighted, maker(target_rows, sources))
    result = lax.map(one_block, target_blocks)
    return result.transpose(1, 0, 2).reshape(weighted.shape[0], target_count)

def reference(points, density, incident, precond, receivers):
    point_count = points.shape[1]
    cell_area = FOUR_PI / point_count
    for iteration in range(ITERS):
        weighted = (density * cell_area).astype(jnp.bfloat16)
        field = blocked(weighted, points, points, single_layer)
        density = density - (field + incident) / precond[None, :]
    weighted = (density * cell_area).astype(jnp.bfloat16)
    toward = receiver_directions(receivers)
    far_field = blocked(weighted, toward, points, far_kernel)
    return (density, far_field)
```

```python
import functools
import math

import jax
import jax.numpy as jnp
import numpy as np
from jax import lax
from jax.experimental import pallas as pl
from jax.experimental.pallas import tpu as pltpu
from jax.sharding import PartitionSpec as P

ITERS = 4
NDIR = 65536
WAVENUMBER = 32.0
SMOOTHING = 0.02
FOUR_PI = 4.0 * math.pi
TURNS = WAVENUMBER / (2.0 * math.pi)
MAGIC = 12582912.0
LANES = 128
CHUNK = 16
MESH = pl.DeviceIdType.MESH
AXES = ("groups", "tgt", "src", "sub")


def cosine_coefficients(degree):
    fit = np.polynomial.chebyshev.Chebyshev.interpolate(
        lambda u: np.cos(2.0 * np.pi * np.sqrt(u)), degree, domain=[0.0, 0.25]
    )
    return [float(c) for c in fit.convert(kind=np.polynomial.Polynomial).coef]


COSINE = cosine_coefficients(6)


def cos_turns(turns, scale=1.0):
    whole = (turns + MAGIC) - MAGIC
    f = turns - whole
    u = f * f
    total = u * (scale * COSINE[-1]) + scale * COSINE[-2]
    for coefficient in COSINE[-3::-1]:
        total = total * u + scale * coefficient
    return total


def directions(number):
    rotation = ((number >> 8) * 14080 + (number & 255) * 40503) & 65535
    part = rotation.astype(jnp.float32) * (1.0 / 65536.0)
    height = 1.0 - (2 * number + 1).astype(jnp.float32) / NDIR
    radial = jnp.sqrt(jnp.maximum(1.0 - height * height, 0.0))
    return radial * cos_turns(part), radial * cos_turns(part - 0.25), height


def kernel(sizes, cell_area, points, density, incident, precond, receivers, out,
           pbuf, w0buf, wbuf, wlast, table, plane, cols, toward, w0out, dloc, iloc, ploc, rloc, dpart, ipart, ppart,
           state, inc, inv, swap_out, swap_in,
           lsem, psend, w0send, wsend, lsend, prcv, w0rcv, wrcv, lrcv, xsend, xrcv):
    density_out, far_out = out.at[0], out.at[1]
    T, S = sizes
    n = T * S
    g, tz, sx, c = (lax.axis_index(a) for a in AXES)
    q = tz * S + sx
    me = 2 * q + c
    other = 1 - c

    def near(j):
        if unroll and isinstance(j, int):
            return dests[j]
        return nearest(jnp.int32(j))

    def nearest(j):
        k, b = lax.div(j, S), lax.rem(j, S)
        inner = jnp.minimum(tz, T - 1 - tz)
        alternating = tz + lax.div(k + 1, 2) * (2 * lax.rem(k, 2) - 1)
        tail = jnp.where(tz <= T - 1 - tz, k, T - 1 - k)
        z = jnp.where(k <= 2 * inner, alternating, tail)
        x = lax.rem(sx + b, S)
        return z, x

    def chip(j):
        z, x = near(j)
        return z * S + x

    unroll = n <= 8
    dests = [nearest(jnp.int32(j)) for j in range(n)] if unroll else []

    def each(start, stop, body):
        if unroll:
            for j in range(start, stop):
                body(j)
        else:
            lax.fori_loop(start, stop, lambda j, z: (body(j), z)[1], 0)

    def sums_of(step, total):
        if unroll:
            for j in range(1, n):
                total = step(j, total)
            return total
        return lax.fori_loop(1, n, step, total)

    loads = [
        pltpu.make_async_copy(points, pbuf.at[me], lsem.at[0]),
        pltpu.make_async_copy(density, dloc, lsem.at[1]),
        pltpu.make_async_copy(incident, iloc, lsem.at[2]),
        pltpu.make_async_copy(precond, ploc, lsem.at[3]),
        pltpu.make_async_copy(receivers.at[me], rloc, lsem.at[4]),
    ]
    for load in loads:
        load.start()

    barrier = pltpu.get_barrier_semaphore()

    def greet(i):
        z, x = near(n - 1 - i)
        for s in range(2):
            pl.semaphore_signal(barrier, inc=1, device_id=(g, z, x, s), device_id_type=MESH)

    each(0, n - 1, greet)
    pl.semaphore_signal(barrier, inc=1, device_id=(g, tz, sx, other), device_id_type=MESH)

    for load in loads:
        load.wait()
    w0 = (dloc[...] * cell_area).astype(jnp.bfloat16)
    w0out[...] = w0
    w0buf[me] = w0out[c]
    pl.semaphore_wait(barrier, 2 * n - 1)

    def first_copy(kind, z, x, s, slot):
        source, target, send, receive = (
            (pbuf.at[me], pbuf.at[me], psend, prcv), (w0out.at[s], w0buf.at[me], w0send, w0rcv))[kind]
        return pltpu.make_async_remote_copy(
            source, target, send.at[slot], receive.at[me], device_id=(g, z, x, s), device_id_type=MESH)

    def start_first(kind, i):
        j = i + 1
        z, x = near(j)
        for s in range(2):
            first_copy(kind, z, x, s, 2 * j + s).start()

    for kind in range(2):
        first_copy(kind, tz, sx, other, 0).start()
        each(0, n - 1, functools.partial(start_first, kind))
    swaps = [
        pltpu.make_async_remote_copy(
            source, target, xsend.at[i], xrcv.at[i], device_id=(g, tz, sx, other), device_id_type=MESH)
        for i, (source, target) in enumerate((
            (dloc.at[other], dpart), (iloc.at[other], ipart), (ploc, ppart)))
    ]
    for copy in swaps:
        copy.start()

    def wait_first(buffer, semaphore, index):
        pltpu.make_async_copy(buffer.at[index], buffer.at[index], semaphore.at[index]).wait()

    def spread(store, half, rows):
        for axis in range(3):
            row = jnp.broadcast_to(rows[axis], (LANES, LANES))
            store[axis, half * LANES:(half + 1) * LANES, :] = row.T

    def build(store, maker, targets, index, scale):
        sources = [pbuf[index + h] * scale for h in range(2)]
        for start in range(0, store.shape[0], CHUNK):
            left = [targets[a, start:start + CHUNK, :] for a in range(3)]
            for h in range(2):
                value = maker(left, [sources[h][a:a + 1, :] for a in range(3)])
                store[start:start + CHUNK, h * LANES:(h + 1) * LANES] = value.astype(jnp.bfloat16)

    def single_layer(targets, sources):
        dx, dy, dz = (t - s for t, s in zip(targets, sources))
        squared = dx * dx + dy * dy + dz * dz
        turns = squared * lax.rsqrt(jnp.maximum(squared, 1e-30))
        return cos_turns(turns, TURNS / FOUR_PI) * lax.rsqrt(squared + (TURNS * SMOOTHING) ** 2)

    def far_kernel(directed, sources):
        turns = directed[0] * sources[0] + directed[1] * sources[1] + directed[2] * sources[2]
        return cos_turns(turns)

    def product(left, right):
        return lax.dot_general(left, right, (((1,), (1,)), ((), ())), preferred_element_type=jnp.float32)

    def ordered(mine, partner):
        first = c == 0
        return jnp.concatenate(
            [jnp.where(first, mine, partner), jnp.where(first, partner, mine)], axis=-1)

    toward_rows = directions(rloc[...])
    spread(toward, 0, [row * TURNS for row in toward_rows])
    wait_first(pbuf, prcv, 2 * q + other)
    for half in range(2):
        spread(cols, half, [pbuf[2 * q + half][a:a + 1] * TURNS for a in range(3)])
    build(table.at[0], single_layer, cols, 2 * q, TURNS)
    for copy in swaps:
        copy.wait_recv()
    state[...] = ordered(dloc[c], dpart[...])
    inc[...] = ordered(iloc[c], ipart[...])
    inv[...] = 1.0 / ordered(ploc[...], ppart[...])

    def table_step(j, carry):
        index = 2 * chip(j)
        wait_first(pbuf, prcv, index)
        wait_first(pbuf, prcv, index + 1)
        build(table.at[j], single_layer, cols, index, TURNS)
        return carry

    def first_product(j, total):
        index = 2 * chip(j)
        weighted = jnp.concatenate([w0buf[index], w0buf[index + 1]], axis=1)
        return total + product(weighted, table[j])

    def first_step(j, total):
        index = 2 * chip(j)
        wait_first(w0buf, w0rcv, index)
        wait_first(w0buf, w0rcv, index + 1)
        return first_product(j, total)

    wait_first(w0buf, w0rcv, 2 * q + other)
    lax.fori_loop(1, n, table_step, 0)
    field = first_product(jnp.int32(0), jnp.zeros((w0out.shape[1], 2 * LANES), jnp.float32))
    field = sums_of(first_step, field)

    def last_copy(z, x, s):
        block = wlast.at[c * n + q]
        return pltpu.make_async_remote_copy(
            block, block, lsend, lrcv.at[c * n + q], device_id=(g, z, x, s), device_id_type=MESH)

    def send_last(cores, i):
        z, x = near(n - 1 - i)
        for s in cores:
            last_copy(z, x, s).start()

    def update(r, total):
        fresh = state[...] - (total + inc[...]) * inv[...]
        weighted = (fresh * cell_area).astype(jnp.bfloat16)
        if r == ITERS - 1:
            wlast[c * n + q] = weighted
            each(0, n - 1, functools.partial(send_last, [0, 1]))
            last_copy(tz, sx, other).start()
            return fresh
        state[...] = fresh
        wbuf[r, q] = weighted

        def send(i):
            z, x = near(n - 1 - i)
            pltpu.make_async_remote_copy(
                wbuf.at[r, q], wbuf.at[r, q], wsend.at[r], wrcv.at[r % 2, q],
                device_id=(g, z, x, c), device_id_type=MESH).start()

        each(0, n - 1, send)
        return fresh

    def plane_step(j, carry):
        index = 2 * chip(j)
        build(plane.at[j], far_kernel, toward, index, 1.0)
        return carry

    def gathered(r):
        def step(j, sums):
            index = chip(j)
            slot = wbuf.at[r, index]
            pltpu.make_async_copy(slot, slot, wrcv.at[r % 2, index]).wait()
            return sums + product(wbuf[r, index], table[j])

        return sums_of(step, product(wbuf[r, q], table[0]))

    def last_wait(index):
        pltpu.make_async_copy(wlast.at[index], wlast.at[index], lrcv.at[index]).wait()

    def far_product(j):
        index = chip(j)
        return product(jnp.concatenate([wlast[index], wlast[n + index]], axis=0), plane[j])

    def far_step(j, sums):
        for s in range(2):
            last_wait(s * n + chip(j))
        return sums + far_product(j)

    share = -(-n // ITERS)
    for r in range(ITERS):
        fresh = update(r, field)
        last = r == ITERS - 1
        if last:
            low, high = fresh[:, :LANES], fresh[:, LANES:]
            swap_out[0] = jnp.where(c == 0, high, low)
            density_out[c] = jnp.where(c == 0, low, high)
            dswap = pltpu.make_async_remote_copy(
                swap_out.at[0], swap_in.at[0], xsend.at[3], xrcv.at[3],
                device_id=(g, tz, sx, other), device_id_type=MESH)
            dswap.start()
        lax.fori_loop(min(r * share, n), min((r + 1) * share, n), plane_step, 0)
        if last:
            dswap.wait_recv()
            density_out[other] = swap_in[0]
            continue
        field = gathered(r)

    def end_first(i):
        z, x = near(i)
        for s in range(2):
            for kind in range(2):
                first_copy(kind, z, x, s, 2 * i + s).wait_send()

    each(1, n, end_first)
    for kind in range(2):
        first_copy(kind, tz, sx, other, 0).wait_send()
    for r in range(ITERS - 1):
        sent = wbuf.at[r, pl.ds(0, n - 1)]
        pltpu.make_async_copy(sent, sent, wsend.at[r]).wait()
    for copy in swaps:
        copy.wait_send()
    dswap.wait_send()

    last_wait(other * n + q)
    far = sums_of(far_step, far_product(0))
    half = far_out.shape[1]
    far_out[0] = far[:half]
    far_out[1] = far[half:]

    sent = wlast.at[pl.ds(0, 2 * n - 1)]
    pltpu.make_async_copy(sent, sent, lsend).wait()


FOLD = np.polynomial.chebyshev.Chebyshev.interpolate(
    lambda v: -np.sin(2.0 * np.pi * np.sqrt(v)) / np.sqrt(v), 3, domain=[0.0, 0.0625]
).convert(kind=np.polynomial.Polynomial).coef
FOLD = [float(c) for c in FOLD]
MONIC = [c / FOLD[3] for c in FOLD[:3]]
KAPPA = (FOUR_PI / (FOLD[3] * TURNS)) ** 2
SOFT = (TURNS * SMOOTHING) ** 2
DEPTH = 32


def folded(turns):
    g = jnp.abs(turns - jnp.round(turns)) - 0.25
    return g, g * g


def parts_of(value):
    high = value.astype(jnp.bfloat16).astype(jnp.float32)
    rest = value - high
    middle = rest.astype(jnp.bfloat16).astype(jnp.float32)
    return high, middle, rest - middle


def stacked(groups):
    return jnp.concatenate(groups + [jnp.zeros_like(groups[0])] * (DEPTH // 4 - len(groups)), axis=0)


def column_kernel(sizes, cell_area, points, density, incident, precond, receivers, out,
                  xloc, dloc, iloc, ploc, rloc, pmsg, pbuf, dmsg, dbuf, left, right, aim, table, plane,
                  state, inc, inv, wfin, wall, dsend, drcv,
                  lsem, psend, prcv, dsnd, drv, tsend, trcv, wsend, wrcv, osend, orcv):
    density_out, far_out = out.at[0], out.at[1]
    T, S = sizes
    n = T * S
    D = 2 * n
    wide = 2 * LANES
    share = dloc.shape[0] // D
    f32, bf16 = jnp.float32, jnp.bfloat16
    g, tz, sx, c = (lax.axis_index(a) for a in AXES)
    q = tz * S + sx
    me = 2 * q + c
    other = 1 - c

    def nearest(j):
        k, b = lax.div(j, S), lax.rem(j, S)
        inner = jnp.minimum(tz, T - 1 - tz)
        alternating = tz + lax.div(k + 1, 2) * (2 * lax.rem(k, 2) - 1)
        tail = jnp.where(tz <= T - 1 - tz, k, T - 1 - k)
        z = jnp.where(k <= 2 * inner, alternating, tail)
        x = lax.rem(sx + b, S)
        return z, x

    dests = [nearest(jnp.int32(j)) for j in range(n)]

    def chip(j):
        z, x = dests[j] if isinstance(j, int) else nearest(j)
        return z * S + x

    peers = [(dests[j], s) for j in range(1, n) for s in range(2)]
    sibling = (dests[0], other)

    def place(peer):
        (z, x), s = peer
        return (g, z, x, s)

    def index_of(peer):
        (z, x), s = peer
        return 2 * (z * S + x) + s

    loads = [
        pltpu.make_async_copy(points, xloc, lsem.at[0]),
        pltpu.make_async_copy(precond, ploc, lsem.at[1]),
        pltpu.make_async_copy(density, dloc, lsem.at[2]),
        pltpu.make_async_copy(incident, iloc, lsem.at[3]),
        pltpu.make_async_copy(receivers.at[me], rloc, lsem.at[4]),
    ]
    for load in loads:
        load.start()
    barrier = pltpu.get_barrier_semaphore()
    for peer in peers[::-1] + [sibling]:
        pl.semaphore_signal(barrier, inc=1, device_id=place(peer), device_id_type=MESH)
    for load in loads:
        load.wait()
    message = jnp.concatenate([xloc[...], 1.0 / ploc[...]], axis=0)
    pmsg[...] = message
    pbuf[me] = message
    for e in range(D):
        rows = slice(share * e, share * (e + 1))
        dmsg[e] = jnp.concatenate([dloc[rows, :], iloc[rows, :]], axis=0)
    dbuf[me] = dmsg[me]
    pl.semaphore_wait(barrier, D - 1)

    def send(source, target, send_sem, receive_sem, peer):
        pltpu.make_async_remote_copy(
            source, target, send_sem, receive_sem, device_id=place(peer), device_id_type=MESH).start()

    def await_in(target, semaphore):
        pltpu.make_async_copy(target, target, semaphore).wait()

    for peer in [sibling] + peers:
        send(pmsg, pbuf.at[me], psend, prcv.at[me], peer)
    for peer in [sibling] + peers:
        send(dmsg.at[index_of(peer)], dbuf.at[me], dsnd, drv.at[me], peer)

    row4 = lax.broadcasted_iota(jnp.int32, (4, wide), 0)
    coordinate = row4 < 3

    def product(a, b):
        return lax.dot_general(a, b, (((1,), (0,)), ((), ())), preferred_element_type=f32)

    def features(j):
        index = 2 * chip(j)
        x = jnp.concatenate([pbuf[index], pbuf[index + 1]], axis=1) * TURNS
        squares = x * x
        a = squares[0:1] + squares[1:2] + squares[2:3]
        high, middle, low = parts_of(jnp.where(coordinate, x, a))
        scale = jnp.where(coordinate, -2.0, 1.0)
        high, middle, low = high * scale, middle * scale, low * scale
        ones = jnp.where(coordinate, 1.0, 0.0)
        left[j] = stacked([high, high, high, middle, middle, low, ones]).T.astype(bf16)
        for h, (factor, shift) in enumerate(((1.0, 0.0), (KAPPA, KAPPA * SOFT))):
            high, middle, low = parts_of(jnp.where(coordinate, x, 1.0) * factor)
            tail = jnp.concatenate(list(parts_of(a * factor + shift)) + [jnp.zeros_like(a)], axis=0)
            right[j, :, h * wide:(h + 1) * wide] = stacked(
                [high, middle, low, high, middle, high, tail]).astype(bf16)

    def entries(pair, diagonal):
        squared, softened = pair[:, :wide], pair[:, wide:]
        if diagonal is not None:
            squared = jnp.where(diagonal, 0.0, squared)
            softened = jnp.where(diagonal, KAPPA * SOFT, softened)
        turns = squared * lax.rsqrt(jnp.maximum(squared, 1e-30))
        fold, v = folded(turns)
        total = ((v + MONIC[2]) * v + MONIC[1]) * v + MONIC[0]
        return (total * fold * lax.rsqrt(softened)).astype(bf16)

    def build(a, blocks):
        for start in range(0, wide, LANES):
            rows = slice(start, start + LANES)
            for b, mirror in blocks:
                diagonal = None
                if not mirror:
                    shape = (LANES, wide)
                    diagonal = lax.broadcasted_iota(jnp.int32, shape, 0) + start == lax.broadcasted_iota(jnp.int32, shape, 1)
                value = entries(product(left[a, rows, :], right[b]), diagonal)
                table[a, b, rows, :] = value
                if mirror:
                    table[b, a, :, rows] = value.T

    def swap(k, m):
        row = 2 * k + c
        block = table.at[row, pl.ds(2 * m, 2)]
        return pltpu.make_async_remote_copy(
            block, block, tsend.at[k, m], trcv.at[k, m], device_id=place(sibling), device_id_type=MESH)

    def swap_own(k):
        row = 2 * k + c
        block = table.at[row, row]
        return pltpu.make_async_remote_copy(
            block, block, tsend.at[k, k], trcv.at[k, k], device_id=place(sibling), device_id_type=MESH)

    rows3 = directions(rloc[...])
    aims = jnp.concatenate(list(rows3) + [jnp.zeros_like(rows3[0])], axis=0) * -0.5
    high, middle, low = parts_of(aims)
    aim[...] = stacked([high, middle, low, high, middle, high]).astype(bf16)

    def step(k, carry):
        for h in range(2):
            j = 2 * k + h
            index = 2 * chip(j)
            for s in range(2):
                @pl.when(index + s != me)
                def _():
                    await_in(pbuf.at[index + s], prcv.at[index + s])
            features(j)

        def across(m, z):
            build(2 * k + c, [(2 * m, True), (2 * m + 1, True)])
            swap(k, m).start()
            return z

        lax.fori_loop(0, k, across, 0)
        build(2 * k + c, [(2 * k + c, False)])
        swap_own(k).start()
        build(2 * k + 1, [(2 * k, True)])
        return carry

    lax.fori_loop(0, n // 2, step, 0)

    state[...] = jnp.zeros_like(state)
    inc[...] = jnp.zeros_like(inc)
    inv[...] = jnp.zeros_like(inv)
    for j in range(n):
        index = 2 * chip(j)
        for s in range(2):
            lanes = slice((2 * j + s) * LANES, (2 * j + s + 1) * LANES)
            if j > 0:
                await_in(dbuf.at[index + s], drv.at[index + s])
            elif s == 0:
                await_in(dbuf.at[2 * q + other], drv.at[2 * q + other])
            message = dbuf[index + s]
            state[0:share, lanes] = message[:share]
            inc[0:share, lanes] = message[share:]
            inv[0:share, lanes] = jnp.broadcast_to(pbuf[index + s][3:4], (share, LANES))

    def mirror_step(k, carry):
        row = 2 * k + other

        def one(m, z):
            await_in(table.at[row, pl.ds(2 * m, 2)], trcv.at[k, m])
            for h in range(2):
                table[2 * m + h, row] = table[row, 2 * m + h].T
            return z

        lax.fori_loop(0, k, one, 0)
        await_in(table.at[row, row], trcv.at[k, k])
        return carry

    lax.fori_loop(0, n // 2, mirror_step, 0)

    def iterate(r, carry):
        weighted = (state[...] * cell_area).astype(bf16)
        for b in range(n):
            lanes = slice(b * wide, (b + 1) * wide)
            field = product(weighted[:, :wide], table[0, b])
            for a in range(1, n):
                field = field + product(weighted[:, a * wide:(a + 1) * wide], table[a, b])
            state[:, lanes] = state[:, lanes] - (field + inc[:, lanes]) * inv[:, lanes]
        return carry

    lax.fori_loop(0, ITERS, iterate, 0)

    weighted = (state[...] * cell_area).astype(bf16)
    for j in range(n):
        wfin[chip(j)] = weighted[0:share, j * wide:(j + 1) * wide]
    for peer in peers[::-1] + [sibling]:
        send(wfin, wall.at[me], wsend, wrcv.at[me], peer)
    for j in range(n):
        for s in range(2):
            dsend[2 * chip(j) + s] = state[0:share, (2 * j + s) * LANES:(2 * j + s + 1) * LANES]
    for peer in peers[::-1] + [sibling]:
        send(dsend.at[index_of(peer)], drcv.at[me], osend, orcv.at[me], peer)
    wall[me] = wfin[...]
    drcv[me] = dsend[me]

    def plane_step(j, carry):
        fold, v = folded(product(left[j], aim[...]))
        total = ((FOLD[3] * v + FOLD[2]) * v + FOLD[1]) * v + FOLD[0]
        plane[j] = (total * fold).astype(bf16)
        return carry

    lax.fori_loop(0, n, plane_step, 0)

    def finish_sends():
        for k in range(n // 2):
            for m in range(k):
                swap(k, m).wait_send()
            swap_own(k).wait_send()
        await_in(pbuf.at[pl.ds(0, D - 1)], psend)
        await_in(dbuf.at[pl.ds(0, D - 1)], dsnd)

    finish_sends()
    for peer in [sibling] + peers:
        index = index_of(peer)
        await_in(wall.at[index], wrcv.at[index])
    for j in range(n):
        index = chip(j)
        gathered = jnp.concatenate([wall[d, index].astype(f32) for d in range(D)], axis=0).astype(bf16)
        part = product(gathered, plane[j])
        far = part if j == 0 else far + part
    half = far_out.shape[1]
    far_out[0] = far[:half]
    far_out[1] = far[half:]
    for peer in [sibling] + peers:
        index = index_of(peer)
        await_in(drcv.at[index], orcv.at[index])
    whole = jnp.concatenate([drcv[d] for d in range(D)], axis=0)
    density_out[0] = whole[:half]
    density_out[1] = whole[half:]
    await_in(wall.at[pl.ds(0, D - 1)], wsend)
    await_in(drcv.at[pl.ds(0, D - 1)], osend)


def column_call(sizes, cell_area, points, density, incident, precond, receivers):
    T, S = sizes
    n = T * S
    D = 2 * n
    columns, own = density.shape
    half = columns // 2
    share = columns // D
    wide = 2 * own
    f32, bf16 = jnp.float32, jnp.bfloat16
    anywhere = pl.BlockSpec(memory_space=pl.ANY)
    dma = pltpu.SemaphoreType.DMA
    return pl.pallas_call(
        functools.partial(column_kernel, sizes, cell_area),
        out_shape=jax.ShapeDtypeStruct((2, 2, half, own), f32),
        in_specs=[anywhere] * 5,
        out_specs=pl.BlockSpec(memory_space=pltpu.VMEM),
        scratch_shapes=[
            pltpu.VMEM((3, own), f32),
            pltpu.VMEM((columns, own), f32),
            pltpu.VMEM((columns, own), f32),
            pltpu.VMEM((1, own), f32),
            pltpu.VMEM((1, own), jnp.int32),
            pltpu.VMEM((4, own), f32),
            pltpu.VMEM((D, 4, own), f32),
            pltpu.VMEM((D, 2 * share, own), f32),
            pltpu.VMEM((D, 2 * share, own), f32),
            pltpu.VMEM((n, wide, DEPTH), bf16),
            pltpu.VMEM((n, DEPTH, 2 * wide), bf16),
            pltpu.VMEM((DEPTH, own), bf16),
            pltpu.VMEM((n, n, wide, wide), bf16),
            pltpu.VMEM((n, wide, own), bf16),
            pltpu.VMEM((8, n * wide), f32),
            pltpu.VMEM((8, n * wide), f32),
            pltpu.VMEM((8, n * wide), f32),
            pltpu.VMEM((n, share, wide), bf16),
            pltpu.VMEM((D, n, share, wide), bf16),
            pltpu.VMEM((D, share, own), f32),
            pltpu.VMEM((D, share, own), f32),
            dma((5,)),
            dma(()),
            dma((D,)),
            dma(()),
            dma((D,)),
            dma((n // 2, n // 2)),
            dma((n // 2, n // 2)),
            dma(()),
            dma((D,)),
            dma(()),
            dma((D,)),
        ],
        compiler_params=pltpu.CompilerParams(
            collective_id=0, has_side_effects=True, vmem_limit_bytes=60 * 1024 * 1024),
    )(
        points, density, incident, precond.reshape(1, own), receivers.reshape(D, 1, own),
    )


def shards(points, density, incident, precond, receivers):
    T, S = lax.axis_size("tgt"), lax.axis_size("src")
    n = T * S
    columns, own = density.shape
    half = columns // 2
    f32, bf16 = jnp.float32, jnp.bfloat16
    cell_area = FOUR_PI / (own * n * 2)
    if n <= 8 and n % 2 == 0 and columns == 4 * n and own == LANES:
        out = column_call((T, S), cell_area, points, density, incident, precond, receivers)
        return out[0].reshape(columns, own), out[1].reshape(columns, own)
    block = pltpu.VMEM((2, 2, half, own), f32)
    anywhere = pl.BlockSpec(memory_space=pl.ANY)
    vmem = pl.BlockSpec(memory_space=pltpu.VMEM)
    dma = pltpu.SemaphoreType.DMA
    out = pl.pallas_call(
        functools.partial(kernel, (T, S), cell_area),
        out_shape=block,
        in_specs=[anywhere] * 5,
        out_specs=vmem,
        scratch_shapes=[
            pltpu.VMEM((2 * n, 3, own), f32),
            pltpu.VMEM((2 * n, half, own), bf16),
            pltpu.VMEM((ITERS - 1, n, half, 2 * own), bf16),
            pltpu.VMEM((2 * n, half, 2 * own), bf16),
            pltpu.VMEM((n, 2 * own, 2 * own), bf16),
            pltpu.VMEM((n, own, 2 * own), bf16),
            pltpu.VMEM((3, 2 * own, own), f32),
            pltpu.VMEM((3, own, own), f32),
            pltpu.VMEM((2, half, own), bf16),
            pltpu.VMEM((2, half, own), f32),
            pltpu.VMEM((2, half, own), f32),
            pltpu.VMEM((1, own), f32),
            pltpu.VMEM((1, own), jnp.int32),
            pltpu.VMEM((half, own), f32),
            pltpu.VMEM((half, own), f32),
            pltpu.VMEM((1, own), f32),
            pltpu.VMEM((half, 2 * own), f32),
            pltpu.VMEM((half, 2 * own), f32),
            pltpu.VMEM((1, 2 * own), f32),
            pltpu.VMEM((1, half, own), f32),
            pltpu.VMEM((1, half, own), f32),
            dma((5,)),
            dma((2 * n,)),
            dma((2 * n,)),
            dma((ITERS - 1,)),
            dma(()),
            dma((2 * n,)),
            dma((2 * n,)),
            dma((2, n)),
            dma((2 * n,)),
            dma((4,)),
            dma((4,)),
        ],
        compiler_params=pltpu.CompilerParams(
            collective_id=0, has_side_effects=True, vmem_limit_bytes=60 * 1024 * 1024),
    )(
        points,
        density.reshape(2, half, own),
        incident.reshape(2, half, own),
        precond.reshape(1, own),
        receivers.reshape(2 * n, 1, own),
    )
    return out[0].reshape(columns, own), out[1].reshape(columns, own)


def solution(mesh):
    split = P(None, AXES)
    return jax.shard_map(
        shards,
        mesh=mesh,
        in_specs=(split, split, split, P(AXES), P("groups")),
        out_specs=(split, split),
        check_vma=False,
    )
```

```python
import functools
import math

import jax
import jax.numpy as jnp
import numpy as np
from jax import lax
from jax.experimental import pallas as pl
from jax.experimental.pallas import tpu as pltpu
from jax.sharding import PartitionSpec as P

ITERS = 4
NDIR = 65536
WAVENUMBER = 32.0
SMOOTHING = 0.02
FOUR_PI = 4.0 * math.pi
TURNS = WAVENUMBER / (2.0 * math.pi)
MAGIC = 12582912.0
LANES = 128
CHUNK = 16
MESH = pl.DeviceIdType.MESH
AXES = ("groups", "tgt", "src", "sub")


def cosine_coefficients(degree):
    fit = np.polynomial.chebyshev.Chebyshev.interpolate(
        lambda u: np.cos(2.0 * np.pi * np.sqrt(u)), degree, domain=[0.0, 0.25]
    )
    return [float(c) for c in fit.convert(kind=np.polynomial.Polynomial).coef]


COSINE = cosine_coefficients(6)


def cos_turns(turns, scale=1.0):
    whole = (turns + MAGIC) - MAGIC
    f = turns - whole
    u = f * f
    total = u * (scale * COSINE[-1]) + scale * COSINE[-2]
    for coefficient in COSINE[-3::-1]:
        total = total * u + scale * coefficient
    return total


def directions(number):
    rotation = ((number >> 8) * 14080 + (number & 255) * 40503) & 65535
    part = rotation.astype(jnp.float32) * (1.0 / 65536.0)
    height = 1.0 - (2 * number + 1).astype(jnp.float32) / NDIR
    radial = jnp.sqrt(jnp.maximum(1.0 - height * height, 0.0))
    return radial * cos_turns(part), radial * cos_turns(part - 0.25), height


def kernel(sizes, cell_area, points, density, incident, precond, receivers, out,
           pbuf, w0buf, wbuf, wlast, table, plane, cols, toward, w0out, dloc, iloc, ploc, rloc, dpart, ipart, ppart,
           state, inc, inv, swap_out, swap_in,
           lsem, psend, w0send, wsend, lsend, prcv, w0rcv, wrcv, lrcv, xsend, xrcv):
    density_out, far_out = out.at[0], out.at[1]
    T, S = sizes
    n = T * S
    g, tz, sx, c = (lax.axis_index(a) for a in AXES)
    q = tz * S + sx
    me = 2 * q + c
    other = 1 - c

    def near(j):
        if unroll and isinstance(j, int):
            return dests[j]
        return nearest(jnp.int32(j))

    def nearest(j):
        k, b = lax.div(j, S), lax.rem(j, S)
        inner = jnp.minimum(tz, T - 1 - tz)
        alternating = tz + lax.div(k + 1, 2) * (2 * lax.rem(k, 2) - 1)
        tail = jnp.where(tz <= T - 1 - tz, k, T - 1 - k)
        z = jnp.where(k <= 2 * inner, alternating, tail)
        x = lax.rem(sx + b, S)
        return z, x

    def chip(j):
        z, x = near(j)
        return z * S + x

    unroll = n <= 8
    dests = [nearest(jnp.int32(j)) for j in range(n)] if unroll else []

    def each(start, stop, body):
        if unroll:
            for j in range(start, stop):
                body(j)
        else:
            lax.fori_loop(start, stop, lambda j, z: (body(j), z)[1], 0)

    def sums_of(step, total):
        if unroll:
            for j in range(1, n):
                total = step(j, total)
            return total
        return lax.fori_loop(1, n, step, total)

    loads = [
        pltpu.make_async_copy(points, pbuf.at[me], lsem.at[0]),
        pltpu.make_async_copy(density, dloc, lsem.at[1]),
        pltpu.make_async_copy(incident, iloc, lsem.at[2]),
        pltpu.make_async_copy(precond, ploc, lsem.at[3]),
        pltpu.make_async_copy(receivers.at[me], rloc, lsem.at[4]),
    ]
    for load in loads:
        load.start()

    barrier = pltpu.get_barrier_semaphore()

    def greet(i):
        z, x = near(n - 1 - i)
        for s in range(2):
            pl.semaphore_signal(barrier, inc=1, device_id=(g, z, x, s), device_id_type=MESH)

    each(0, n - 1, greet)
    pl.semaphore_signal(barrier, inc=1, device_id=(g, tz, sx, other), device_id_type=MESH)

    for load in loads:
        load.wait()
    w0 = (dloc[...] * cell_area).astype(jnp.bfloat16)
    w0out[...] = w0
    w0buf[me] = w0out[c]
    pl.semaphore_wait(barrier, 2 * n - 1)

    def first_copy(kind, z, x, s, slot):
        source, target, send, receive = (
            (pbuf.at[me], pbuf.at[me], psend, prcv), (w0out.at[s], w0buf.at[me], w0send, w0rcv))[kind]
        return pltpu.make_async_remote_copy(
            source, target, send.at[slot], receive.at[me], device_id=(g, z, x, s), device_id_type=MESH)

    def start_first(kind, i):
        j = i + 1
        z, x = near(j)
        for s in range(2):
            first_copy(kind, z, x, s, 2 * j + s).start()

    for kind in range(2):
        first_copy(kind, tz, sx, other, 0).start()
        each(0, n - 1, functools.partial(start_first, kind))
    swaps = [
        pltpu.make_async_remote_copy(
            source, target, xsend.at[i], xrcv.at[i], device_id=(g, tz, sx, other), device_id_type=MESH)
        for i, (source, target) in enumerate((
            (dloc.at[other], dpart), (iloc.at[other], ipart), (ploc, ppart)))
    ]
    for copy in swaps:
        copy.start()

    def wait_first(buffer, semaphore, index):
        pltpu.make_async_copy(buffer.at[index], buffer.at[index], semaphore.at[index]).wait()

    def spread(store, half, rows):
        for axis in range(3):
            row = jnp.broadcast_to(rows[axis], (LANES, LANES))
            store[axis, half * LANES:(half + 1) * LANES, :] = row.T

    def build(store, maker, targets, index, scale):
        sources = [pbuf[index + h] * scale for h in range(2)]
        for start in range(0, store.shape[0], CHUNK):
            left = [targets[a, start:start + CHUNK, :] for a in range(3)]
            for h in range(2):
                value = maker(left, [sources[h][a:a + 1, :] for a in range(3)])
                store[start:start + CHUNK, h * LANES:(h + 1) * LANES] = value.astype(jnp.bfloat16)

    def single_layer(targets, sources):
        dx, dy, dz = (t - s for t, s in zip(targets, sources))
        squared = dx * dx + dy * dy + dz * dz
        turns = squared * lax.rsqrt(jnp.maximum(squared, 1e-30))
        return cos_turns(turns, TURNS / FOUR_PI) * lax.rsqrt(squared + (TURNS * SMOOTHING) ** 2)

    def far_kernel(directed, sources):
        turns = directed[0] * sources[0] + directed[1] * sources[1] + directed[2] * sources[2]
        return cos_turns(turns)

    def product(left, right):
        return lax.dot_general(left, right, (((1,), (1,)), ((), ())), preferred_element_type=jnp.float32)

    def ordered(mine, partner):
        first = c == 0
        return jnp.concatenate(
            [jnp.where(first, mine, partner), jnp.where(first, partner, mine)], axis=-1)

    toward_rows = directions(rloc[...])
    spread(toward, 0, [row * TURNS for row in toward_rows])
    wait_first(pbuf, prcv, 2 * q + other)
    for half in range(2):
        spread(cols, half, [pbuf[2 * q + half][a:a + 1] * TURNS for a in range(3)])
    build(table.at[0], single_layer, cols, 2 * q, TURNS)
    for copy in swaps:
        copy.wait_recv()
    state[...] = ordered(dloc[c], dpart[...])
    inc[...] = ordered(iloc[c], ipart[...])
    inv[...] = 1.0 / ordered(ploc[...], ppart[...])

    def table_step(j, carry):
        index = 2 * chip(j)
        wait_first(pbuf, prcv, index)
        wait_first(pbuf, prcv, index + 1)
        build(table.at[j], single_layer, cols, index, TURNS)
        return carry

    def first_product(j, total):
        index = 2 * chip(j)
        weighted = jnp.concatenate([w0buf[index], w0buf[index + 1]], axis=1)
        return total + product(weighted, table[j])

    def first_step(j, total):
        index = 2 * chip(j)
        wait_first(w0buf, w0rcv, index)
        wait_first(w0buf, w0rcv, index + 1)
        return first_product(j, total)

    wait_first(w0buf, w0rcv, 2 * q + other)
    lax.fori_loop(1, n, table_step, 0)
    field = first_product(jnp.int32(0), jnp.zeros((w0out.shape[1], 2 * LANES), jnp.float32))
    field = sums_of(first_step, field)

    def last_copy(z, x, s):
        block = wlast.at[c * n + q]
        return pltpu.make_async_remote_copy(
            block, block, lsend, lrcv.at[c * n + q], device_id=(g, z, x, s), device_id_type=MESH)

    def send_last(cores, i):
        z, x = near(n - 1 - i)
        for s in cores:
            last_copy(z, x, s).start()

    def update(r, total):
        fresh = state[...] - (total + inc[...]) * inv[...]
        weighted = (fresh * cell_area).astype(jnp.bfloat16)
        if r == ITERS - 1:
            wlast[c * n + q] = weighted
            each(0, n - 1, functools.partial(send_last, [0, 1]))
            last_copy(tz, sx, other).start()
            return fresh
        state[...] = fresh
        wbuf[r, q] = weighted

        def send(i):
            z, x = near(n - 1 - i)
            pltpu.make_async_remote_copy(
                wbuf.at[r, q], wbuf.at[r, q], wsend.at[r], wrcv.at[r % 2, q],
                device_id=(g, z, x, c), device_id_type=MESH).start()

        each(0, n - 1, send)
        return fresh

    def plane_step(j, carry):
        index = 2 * chip(j)
        build(plane.at[j], far_kernel, toward, index, 1.0)
        return carry

    def gathered(r):
        def step(j, sums):
            index = chip(j)
            slot = wbuf.at[r, index]
            pltpu.make_async_copy(slot, slot, wrcv.at[r % 2, index]).wait()
            return sums + product(wbuf[r, index], table[j])

        return sums_of(step, product(wbuf[r, q], table[0]))

    def last_wait(index):
        pltpu.make_async_copy(wlast.at[index], wlast.at[index], lrcv.at[index]).wait()

    def far_product(j):
        index = chip(j)
        return product(jnp.concatenate([wlast[index], wlast[n + index]], axis=0), plane[j])

    def far_step(j, sums):
        for s in range(2):
            last_wait(s * n + chip(j))
        return sums + far_product(j)

    share = -(-n // ITERS)
    for r in range(ITERS):
        fresh = update(r, field)
        last = r == ITERS - 1
        if last:
            low, high = fresh[:, :LANES], fresh[:, LANES:]
            swap_out[0] = jnp.where(c == 0, high, low)
            density_out[c] = jnp.where(c == 0, low, high)
            dswap = pltpu.make_async_remote_copy(
                swap_out.at[0], swap_in.at[0], xsend.at[3], xrcv.at[3],
                device_id=(g, tz, sx, other), device_id_type=MESH)
            dswap.start()
        lax.fori_loop(min(r * share, n), min((r + 1) * share, n), plane_step, 0)
        if last:
            dswap.wait_recv()
            density_out[other] = swap_in[0]
            continue
        field = gathered(r)

    def end_first(i):
        z, x = near(i)
        for s in range(2):
            for kind in range(2):
                first_copy(kind, z, x, s, 2 * i + s).wait_send()

    each(1, n, end_first)
    for kind in range(2):
        first_copy(kind, tz, sx, other, 0).wait_send()
    for r in range(ITERS - 1):
        sent = wbuf.at[r, pl.ds(0, n - 1)]
        pltpu.make_async_copy(sent, sent, wsend.at[r]).wait()
    for copy in swaps:
        copy.wait_send()
    dswap.wait_send()

    last_wait(other * n + q)
    far = sums_of(far_step, far_product(0))
    half = far_out.shape[1]
    far_out[0] = far[:half]
    far_out[1] = far[half:]

    sent = wlast.at[pl.ds(0, 2 * n - 1)]
    pltpu.make_async_copy(sent, sent, lsend).wait()


FOLD = np.polynomial.chebyshev.Chebyshev.interpolate(
    lambda v: -np.sin(2.0 * np.pi * np.sqrt(v)) / np.sqrt(v), 3, domain=[0.0, 0.0625]
).convert(kind=np.polynomial.Polynomial).coef
FOLD = [float(c) for c in FOLD]
MONIC = [c / FOLD[3] for c in FOLD[:3]]
KAPPA = (FOUR_PI / (FOLD[3] * TURNS)) ** 2
SOFT = (TURNS * SMOOTHING) ** 2
DEPTH = 32
ROWS = 64


def folded(turns):
    g = jnp.abs(turns - jnp.round(turns)) - 0.25
    return g, g * g


def parts_of(value):
    high = value.astype(jnp.bfloat16).astype(jnp.float32)
    rest = value - high
    middle = rest.astype(jnp.bfloat16).astype(jnp.float32)
    return high, middle, rest - middle


def stacked(groups):
    return jnp.concatenate(groups + [jnp.zeros_like(groups[0])] * (DEPTH // 4 - len(groups)), axis=0)


def column_kernel(sizes, cell_area, points, density, incident, precond, receivers, out,
                  xloc, dloc, iloc, ploc, rloc, pmsg, pbuf, dmsg, dbuf, left, right, aim, stage, table, plane,
                  state, inc, inv, wfin, wall, dsend, drcv,
                  lsem, psend, prcv, dsnd, drv, tsend, trcv, wsend, wrcv, osend, orcv):
    density_out, far_out = out.at[0], out.at[1]
    T, S = sizes
    n = T * S
    D = 2 * n
    wide = 2 * LANES
    share = dloc.shape[0] // D
    f32, bf16 = jnp.float32, jnp.bfloat16
    g, tz, sx, c = (lax.axis_index(a) for a in AXES)
    q = tz * S + sx
    me = 2 * q + c
    other = 1 - c

    def nearest(j):
        k, b = lax.div(j, S), lax.rem(j, S)
        inner = jnp.minimum(tz, T - 1 - tz)
        alternating = tz + lax.div(k + 1, 2) * (2 * lax.rem(k, 2) - 1)
        tail = jnp.where(tz <= T - 1 - tz, k, T - 1 - k)
        z = jnp.where(k <= 2 * inner, alternating, tail)
        x = lax.rem(sx + b, S)
        return z, x

    dests = [nearest(jnp.int32(j)) for j in range(n)]

    spots = []
    for k in range(n // 2):
        for h in (c, other):
            z, x = nearest(2 * k + h)
            spots.append(z * S + x)

    peers = [(dests[j], s) for j in range(1, n) for s in range(2)]
    sibling = (dests[0], other)

    def place(peer):
        (z, x), s = peer
        return (g, z, x, s)

    def index_of(peer):
        (z, x), s = peer
        return 2 * (z * S + x) + s

    loads = [
        pltpu.make_async_copy(points, xloc, lsem.at[0]),
        pltpu.make_async_copy(precond, ploc, lsem.at[1]),
        pltpu.make_async_copy(density, dloc, lsem.at[2]),
        pltpu.make_async_copy(incident, iloc, lsem.at[3]),
        pltpu.make_async_copy(receivers.at[me], rloc, lsem.at[4]),
    ]
    for load in loads:
        load.start()
    barrier = pltpu.get_barrier_semaphore()
    for peer in peers[::-1] + [sibling]:
        pl.semaphore_signal(barrier, inc=1, device_id=place(peer), device_id_type=MESH)
    for load in loads:
        load.wait()
    message = jnp.concatenate([xloc[...], 1.0 / ploc[...]], axis=0)
    pmsg[...] = message
    pbuf[me] = message
    for e in range(D):
        rows = slice(share * e, share * (e + 1))
        dmsg[e] = jnp.concatenate([dloc[rows, :], iloc[rows, :]], axis=0)
    dbuf[me] = dmsg[me]
    pl.semaphore_wait(barrier, D - 1)

    def send(source, target, send_sem, receive_sem, peer):
        pltpu.make_async_remote_copy(
            source, target, send_sem, receive_sem, device_id=place(peer), device_id_type=MESH).start()

    def await_in(target, semaphore):
        pltpu.make_async_copy(target, target, semaphore).wait()

    for peer in [sibling] + peers:
        send(pmsg, pbuf.at[me], psend, prcv.at[tz], peer)
    for peer in [sibling] + peers:
        send(dmsg.at[index_of(peer)], dbuf.at[me], dsnd, drv, peer)

    row4 = lax.broadcasted_iota(jnp.int32, (4, wide), 0)
    coordinate = row4 < 3

    def product(a, b):
        return lax.dot_general(a, b, (((1,), (0,)), ((), ())), preferred_element_type=f32)

    def features(p):
        index = 2 * spots[p]
        x = jnp.concatenate([pbuf[index], pbuf[index + 1]], axis=1) * TURNS
        squares = x * x
        a = squares[0:1] + squares[1:2] + squares[2:3]
        high, middle, low = parts_of(jnp.where(coordinate, x, a))
        scale = jnp.where(coordinate, -2.0, 1.0)
        high, middle, low = high * scale, middle * scale, low * scale
        ones = jnp.where(coordinate, 1.0, 0.0)
        left[p] = stacked([high, high, high, middle, middle, low, ones]).T.astype(bf16)
        for h, (factor, shift) in enumerate(((1.0, 0.0), (KAPPA, KAPPA * SOFT))):
            high, middle, low = parts_of(jnp.where(coordinate, x, 1.0) * factor)
            tail = jnp.concatenate(list(parts_of(a * factor + shift)) + [jnp.zeros_like(a)], axis=0)
            right[p, :, h * wide:(h + 1) * wide] = stacked(
                [high, middle, low, high, middle, high, tail]).astype(bf16)

    def entries(pair, diagonal):
        squared, softened = pair[:, :wide], pair[:, wide:]
        if diagonal is not None:
            squared = jnp.where(diagonal, 0.0, squared)
            softened = jnp.where(diagonal, KAPPA * SOFT, softened)
        turns = squared * lax.rsqrt(jnp.maximum(squared, 1e-30))
        fold, v = folded(turns)
        total = ((v + MONIC[2]) * v + MONIC[1]) * v + MONIC[0]
        return (total * fold * lax.rsqrt(softened)).astype(bf16)

    def distances(unit, slot):
        for i, (a, b) in enumerate(unit):
            stage[slot, i] = product(left[a], right[b])

    def shade(unit, slot):
        for start in range(0, wide, ROWS):
            rows = slice(start, start + ROWS)
            for i, (a, b) in enumerate(unit):
                diagonal = None
                if a == b:
                    shape = (ROWS, wide)
                    diagonal = lax.broadcasted_iota(jnp.int32, shape, 0) + start == lax.broadcasted_iota(jnp.int32, shape, 1)
                table[a, b, rows, :] = entries(stage[slot, i, rows, :], diagonal)

    def swap(k, b):
        return pltpu.make_async_remote_copy(
            table.at[2 * k, b], table.at[2 * k + 1, b ^ 1], tsend.at[k], trcv.at[k],
            device_id=place(sibling), device_id_type=MESH)

    def flip(a, b):
        table[b, a] = table[a, b].T

    def swapped(k):
        return table.at[0, pl.ds(0, 2 * k + 1)]

    rows3 = directions(rloc[...])
    aims = jnp.concatenate(list(rows3) + [jnp.zeros_like(rows3[0])], axis=0) * -0.5
    high, middle, low = parts_of(aims)
    aim[...] = stacked([high, middle, low, high, middle, high]).astype(bf16)

    def plane_in(k):
        count = 4 if k else 3
        await_in(pbuf.at[pl.ds(0, count)], prcv.at[dests[2 * k][0]])
        features(2 * k)
        features(2 * k + 1)

    def columns_in():
        await_in(dbuf.at[pl.ds(0, D - 1)], drv)
        state[...] = jnp.zeros_like(state)
        inc[...] = jnp.zeros_like(inc)
        inv[...] = jnp.zeros_like(inv)
        for p in range(n):
            for s in range(2):
                index = 2 * spots[p] + s
                lanes = slice((2 * p + s) * LANES, (2 * p + s + 1) * LANES)
                message = dbuf[index]
                state[0:share, lanes] = message[:share]
                inc[0:share, lanes] = message[share:]
                inv[0:share, lanes] = jnp.broadcast_to(pbuf[index][3:4], (share, LANES))

    units = []
    for k in range(n // 2):
        units += [(k, [(2 * k, 2 * m), (2 * k, 2 * m + 1)]) for m in range(k)]
        units += [(k, [(2 * k, 2 * k), (2 * k + 1, 2 * k)])]
    last = n // 2 - 1
    plane_in(0)
    distances(units[0][1], 0)
    flips = []
    for i, (k, unit) in enumerate(units):
        following = units[i + 1] if i + 1 < len(units) else None
        if following and following[0] != k:
            plane_in(following[0])
        if unit[0][0] == unit[0][1]:
            for old in [k - 1] if k else []:
                await_in(swapped(old), trcv.at[old])
                flips += [(2 * old + 1, b) for b in range(2 * old)]
        for a, b in flips:
            flip(a, b)
        if following:
            distances(following[1], (i + 1) % 2)
        shade(unit, i % 2)
        flips = [(a, b) for a, b in unit if a != b]
        for a, b in unit:
            if a == 2 * k:
                swap(k, b).start()
        if i == len(units) - 2:
            columns_in()
    for a, b in flips:
        flip(a, b)

    def piece(value, p):
        return value[:, p * wide:(p + 1) * wide]

    def gather_field(weighted, sources, b):
        total = None
        for a in sources:
            part = product(piece(weighted, a), table[a, b])
            total = part if total is None else total + part
        return total

    def update(field, b):
        lanes = slice(b * wide, (b + 1) * wide)
        state[:, lanes] = state[:, lanes] - (field + inc[:, lanes]) * inv[:, lanes]

    weighted = (state[...] * cell_area).astype(bf16)
    fields = [gather_field(weighted, range(n - 1), b) for b in range(n - 1)]
    await_in(swapped(last), trcv.at[last])
    for b in range(n - 2):
        flip(n - 1, b)
    for b in range(n - 1):
        update(fields[b] + product(piece(weighted, n - 1), table[n - 1, b]), b)
    update(gather_field(weighted, range(n), n - 1), n - 1)

    def iterate(r, carry):
        weighted = (state[...] * cell_area).astype(bf16)
        for b in range(n):
            update(gather_field(weighted, range(n), b), b)
        return carry

    lax.fori_loop(1, ITERS, iterate, 0)

    weighted = (state[...] * cell_area).astype(bf16)
    for p in range(n):
        wfin[spots[p]] = weighted[0:share, p * wide:(p + 1) * wide]
    for peer in peers[::-1] + [sibling]:
        send(wfin, wall.at[me], wsend, wrcv, peer)
    for p in range(n):
        for s in range(2):
            dsend[2 * spots[p] + s] = state[0:share, (2 * p + s) * LANES:(2 * p + s + 1) * LANES]
    for peer in peers[::-1] + [sibling]:
        send(dsend.at[index_of(peer)], drcv.at[me], osend, orcv, peer)
    wall[me] = wfin[...]
    drcv[me] = dsend[me]

    def plane_step(j, carry):
        fold, v = folded(product(left[j], aim[...]))
        total = ((FOLD[3] * v + FOLD[2]) * v + FOLD[1]) * v + FOLD[0]
        plane[j] = (total * fold).astype(bf16)
        return carry

    lax.fori_loop(0, n, plane_step, 0)

    def finish_sends():
        for k in range(n // 2):
            await_in(swapped(k), tsend.at[k])
        await_in(pbuf.at[pl.ds(0, D - 1)], psend)
        await_in(dbuf.at[pl.ds(0, D - 1)], dsnd)

    finish_sends()
    await_in(wall.at[pl.ds(0, D - 1)], wrcv)
    for j in range(n):
        index = spots[j]
        gathered = jnp.concatenate([wall[d, index].astype(f32) for d in range(D)], axis=0).astype(bf16)
        part = product(gathered, plane[j])
        far = part if j == 0 else far + part
    half = far_out.shape[1]
    far_out[0] = far[:half]
    far_out[1] = far[half:]
    await_in(drcv.at[pl.ds(0, D - 1)], orcv)
    whole = jnp.concatenate([drcv[d] for d in range(D)], axis=0)
    density_out[0] = whole[:half]
    density_out[1] = whole[half:]
    await_in(wall.at[pl.ds(0, D - 1)], wsend)
    await_in(drcv.at[pl.ds(0, D - 1)], osend)


def column_call(sizes, cell_area, points, density, incident, precond, receivers):
    T, S = sizes
    n = T * S
    D = 2 * n
    columns, own = density.shape
    half = columns // 2
    share = columns // D
    wide = 2 * own
    f32, bf16 = jnp.float32, jnp.bfloat16
    anywhere = pl.BlockSpec(memory_space=pl.ANY)
    dma = pltpu.SemaphoreType.DMA
    return pl.pallas_call(
        functools.partial(column_kernel, sizes, cell_area),
        out_shape=jax.ShapeDtypeStruct((2, 2, half, own), f32),
        in_specs=[anywhere] * 5,
        out_specs=pl.BlockSpec(memory_space=pltpu.VMEM),
        scratch_shapes=[
            pltpu.VMEM((3, own), f32),
            pltpu.VMEM((columns, own), f32),
            pltpu.VMEM((columns, own), f32),
            pltpu.VMEM((1, own), f32),
            pltpu.VMEM((1, own), jnp.int32),
            pltpu.VMEM((4, own), f32),
            pltpu.VMEM((D, 4, own), f32),
            pltpu.VMEM((D, 2 * share, own), f32),
            pltpu.VMEM((D, 2 * share, own), f32),
            pltpu.VMEM((n, wide, DEPTH), bf16),
            pltpu.VMEM((n, DEPTH, 2 * wide), bf16),
            pltpu.VMEM((DEPTH, own), bf16),
            pltpu.VMEM((2, 2, wide, 2 * wide), f32),
            pltpu.VMEM((n, n, wide, wide), bf16),
            pltpu.VMEM((n, wide, own), bf16),
            pltpu.VMEM((8, n * wide), f32),
            pltpu.VMEM((8, n * wide), f32),
            pltpu.VMEM((8, n * wide), f32),
            pltpu.VMEM((n, share, wide), bf16),
            pltpu.VMEM((D, n, share, wide), bf16),
            pltpu.VMEM((D, share, own), f32),
            pltpu.VMEM((D, share, own), f32),
            dma((5,)),
            dma(()),
            dma((T,)),
            dma(()),
            dma(()),
            dma((n // 2,)),
            dma((n // 2,)),
            dma(()),
            dma(()),
            dma(()),
            dma(()),
        ],
        compiler_params=pltpu.CompilerParams(
            collective_id=0, has_side_effects=True, vmem_limit_bytes=60 * 1024 * 1024),
    )(
        points, density, incident, precond.reshape(1, own), receivers.reshape(D, 1, own),
    )


def shards(points, density, incident, precond, receivers):
    T, S = lax.axis_size("tgt"), lax.axis_size("src")
    n = T * S
    columns, own = density.shape
    half = columns // 2
    f32, bf16 = jnp.float32, jnp.bfloat16
    cell_area = FOUR_PI / (own * n * 2)
    if S == 2 and n <= 8 and columns == 4 * n and own == LANES:
        out = column_call((T, S), cell_area, points, density, incident, precond, receivers)
        return out[0].reshape(columns, own), out[1].reshape(columns, own)
    block = pltpu.VMEM((2, 2, half, own), f32)
    anywhere = pl.BlockSpec(memory_space=pl.ANY)
    vmem = pl.BlockSpec(memory_space=pltpu.VMEM)
    dma = pltpu.SemaphoreType.DMA
    out = pl.pallas_call(
        functools.partial(kernel, (T, S), cell_area),
        out_shape=block,
        in_specs=[anywhere] * 5,
        out_specs=vmem,
        scratch_shapes=[
            pltpu.VMEM((2 * n, 3, own), f32),
            pltpu.VMEM((2 * n, half, own), bf16),
            pltpu.VMEM((ITERS - 1, n, half, 2 * own), bf16),
            pltpu.VMEM((2 * n, half, 2 * own), bf16),
            pltpu.VMEM((n, 2 * own, 2 * own), bf16),
            pltpu.VMEM((n, own, 2 * own), bf16),
            pltpu.VMEM((3, 2 * own, own), f32),
            pltpu.VMEM((3, own, own), f32),
            pltpu.VMEM((2, half, own), bf16),
            pltpu.VMEM((2, half, own), f32),
            pltpu.VMEM((2, half, own), f32),
            pltpu.VMEM((1, own), f32),
            pltpu.VMEM((1, own), jnp.int32),
            pltpu.VMEM((half, own), f32),
            pltpu.VMEM((half, own), f32),
            pltpu.VMEM((1, own), f32),
            pltpu.VMEM((half, 2 * own), f32),
            pltpu.VMEM((half, 2 * own), f32),
            pltpu.VMEM((1, 2 * own), f32),
            pltpu.VMEM((1, half, own), f32),
            pltpu.VMEM((1, half, own), f32),
            dma((5,)),
            dma((2 * n,)),
            dma((2 * n,)),
            dma((ITERS - 1,)),
            dma(()),
            dma((2 * n,)),
            dma((2 * n,)),
            dma((2, n)),
            dma((2 * n,)),
            dma((4,)),
            dma((4,)),
        ],
        compiler_params=pltpu.CompilerParams(
            collective_id=0, has_side_effects=True, vmem_limit_bytes=60 * 1024 * 1024),
    )(
        points,
        density.reshape(2, half, own),
        incident.reshape(2, half, own),
        precond.reshape(1, own),
        receivers.reshape(2 * n, 1, own),
    )
    return out[0].reshape(columns, own), out[1].reshape(columns, own)


def solution(mesh):
    split = P(None, AXES)
    return jax.shard_map(
        shards,
        mesh=mesh,
        in_specs=(split, split, split, P(AXES), P("groups")),
        out_specs=(split, split),
        check_vma=False,
    )
```

```python
import functools
import math

import jax
import jax.numpy as jnp
import numpy as np
from jax import lax
from jax.experimental import pallas as pl
from jax.experimental.pallas import tpu as pltpu
from jax.sharding import PartitionSpec as P

ITERS = 4
NDIR = 65536
WAVENUMBER = 32.0
SMOOTHING = 0.02
FOUR_PI = 4.0 * math.pi
TURNS = WAVENUMBER / (2.0 * math.pi)
MAGIC = 12582912.0
LANES = 128
CHUNK = 16
MESH = pl.DeviceIdType.MESH
AXES = ("groups", "tgt", "src", "sub")


def cosine_coefficients(degree):
    fit = np.polynomial.chebyshev.Chebyshev.interpolate(
        lambda u: np.cos(2.0 * np.pi * np.sqrt(u)), degree, domain=[0.0, 0.25]
    )
    return [float(c) for c in fit.convert(kind=np.polynomial.Polynomial).coef]


COSINE = cosine_coefficients(6)


def cos_turns(turns, scale=1.0):
    whole = (turns + MAGIC) - MAGIC
    f = turns - whole
    u = f * f
    total = u * (scale * COSINE[-1]) + scale * COSINE[-2]
    for coefficient in COSINE[-3::-1]:
        total = total * u + scale * coefficient
    return total


def directions(number):
    rotation = ((number >> 8) * 14080 + (number & 255) * 40503) & 65535
    part = rotation.astype(jnp.float32) * (1.0 / 65536.0)
    height = 1.0 - (2 * number + 1).astype(jnp.float32) / NDIR
    radial = jnp.sqrt(jnp.maximum(1.0 - height * height, 0.0))
    return radial * cos_turns(part), radial * cos_turns(part - 0.25), height


def kernel(sizes, cell_area, points, density, incident, precond, receivers, out,
           pbuf, w0buf, wbuf, wlast, table, plane, cols, toward, w0out, dloc, iloc, ploc, rloc, dpart, ipart, ppart,
           state, inc, inv, swap_out, swap_in,
           lsem, psend, w0send, wsend, lsend, prcv, w0rcv, wrcv, lrcv, xsend, xrcv):
    density_out, far_out = out.at[0], out.at[1]
    T, S = sizes
    n = T * S
    g, tz, sx, c = (lax.axis_index(a) for a in AXES)
    q = tz * S + sx
    me = 2 * q + c
    other = 1 - c

    def near(j):
        if unroll and isinstance(j, int):
            return dests[j]
        return nearest(jnp.int32(j))

    def nearest(j):
        k, b = lax.div(j, S), lax.rem(j, S)
        inner = jnp.minimum(tz, T - 1 - tz)
        alternating = tz + lax.div(k + 1, 2) * (2 * lax.rem(k, 2) - 1)
        tail = jnp.where(tz <= T - 1 - tz, k, T - 1 - k)
        z = jnp.where(k <= 2 * inner, alternating, tail)
        x = lax.rem(sx + b, S)
        return z, x

    def chip(j):
        z, x = near(j)
        return z * S + x

    unroll = n <= 8
    dests = [nearest(jnp.int32(j)) for j in range(n)] if unroll else []

    def each(start, stop, body):
        if unroll:
            for j in range(start, stop):
                body(j)
        else:
            lax.fori_loop(start, stop, lambda j, z: (body(j), z)[1], 0)

    def sums_of(step, total):
        if unroll:
            for j in range(1, n):
                total = step(j, total)
            return total
        return lax.fori_loop(1, n, step, total)

    loads = [
        pltpu.make_async_copy(points, pbuf.at[me], lsem.at[0]),
        pltpu.make_async_copy(density, dloc, lsem.at[1]),
        pltpu.make_async_copy(incident, iloc, lsem.at[2]),
        pltpu.make_async_copy(precond, ploc, lsem.at[3]),
        pltpu.make_async_copy(receivers.at[me], rloc, lsem.at[4]),
    ]
    for load in loads:
        load.start()

    barrier = pltpu.get_barrier_semaphore()

    def greet(i):
        z, x = near(n - 1 - i)
        for s in range(2):
            pl.semaphore_signal(barrier, inc=1, device_id=(g, z, x, s), device_id_type=MESH)

    each(0, n - 1, greet)
    pl.semaphore_signal(barrier, inc=1, device_id=(g, tz, sx, other), device_id_type=MESH)

    for load in loads:
        load.wait()
    w0 = (dloc[...] * cell_area).astype(jnp.bfloat16)
    w0out[...] = w0
    w0buf[me] = w0out[c]
    pl.semaphore_wait(barrier, 2 * n - 1)

    def first_copy(kind, z, x, s, slot):
        source, target, send, receive = (
            (pbuf.at[me], pbuf.at[me], psend, prcv), (w0out.at[s], w0buf.at[me], w0send, w0rcv))[kind]
        return pltpu.make_async_remote_copy(
            source, target, send.at[slot], receive.at[me], device_id=(g, z, x, s), device_id_type=MESH)

    def start_first(kind, i):
        j = i + 1
        z, x = near(j)
        for s in range(2):
            first_copy(kind, z, x, s, 2 * j + s).start()

    for kind in range(2):
        first_copy(kind, tz, sx, other, 0).start()
        each(0, n - 1, functools.partial(start_first, kind))
    swaps = [
        pltpu.make_async_remote_copy(
            source, target, xsend.at[i], xrcv.at[i], device_id=(g, tz, sx, other), device_id_type=MESH)
        for i, (source, target) in enumerate((
            (dloc.at[other], dpart), (iloc.at[other], ipart), (ploc, ppart)))
    ]
    for copy in swaps:
        copy.start()

    def wait_first(buffer, semaphore, index):
        pltpu.make_async_copy(buffer.at[index], buffer.at[index], semaphore.at[index]).wait()

    def spread(store, half, rows):
        for axis in range(3):
            row = jnp.broadcast_to(rows[axis], (LANES, LANES))
            store[axis, half * LANES:(half + 1) * LANES, :] = row.T

    def build(store, maker, targets, index, scale):
        sources = [pbuf[index + h] * scale for h in range(2)]
        for start in range(0, store.shape[0], CHUNK):
            left = [targets[a, start:start + CHUNK, :] for a in range(3)]
            for h in range(2):
                value = maker(left, [sources[h][a:a + 1, :] for a in range(3)])
                store[start:start + CHUNK, h * LANES:(h + 1) * LANES] = value.astype(jnp.bfloat16)

    def single_layer(targets, sources):
        dx, dy, dz = (t - s for t, s in zip(targets, sources))
        squared = dx * dx + dy * dy + dz * dz
        turns = squared * lax.rsqrt(jnp.maximum(squared, 1e-30))
        return cos_turns(turns, TURNS / FOUR_PI) * lax.rsqrt(squared + (TURNS * SMOOTHING) ** 2)

    def far_kernel(directed, sources):
        turns = directed[0] * sources[0] + directed[1] * sources[1] + directed[2] * sources[2]
        return cos_turns(turns)

    def product(left, right):
        return lax.dot_general(left, right, (((1,), (1,)), ((), ())), preferred_element_type=jnp.float32)

    def ordered(mine, partner):
        first = c == 0
        return jnp.concatenate(
            [jnp.where(first, mine, partner), jnp.where(first, partner, mine)], axis=-1)

    toward_rows = directions(rloc[...])
    spread(toward, 0, [row * TURNS for row in toward_rows])
    wait_first(pbuf, prcv, 2 * q + other)
    for half in range(2):
        spread(cols, half, [pbuf[2 * q + half][a:a + 1] * TURNS for a in range(3)])
    build(table.at[0], single_layer, cols, 2 * q, TURNS)
    for copy in swaps:
        copy.wait_recv()
    state[...] = ordered(dloc[c], dpart[...])
    inc[...] = ordered(iloc[c], ipart[...])
    inv[...] = 1.0 / ordered(ploc[...], ppart[...])

    def table_step(j, carry):
        index = 2 * chip(j)
        wait_first(pbuf, prcv, index)
        wait_first(pbuf, prcv, index + 1)
        build(table.at[j], single_layer, cols, index, TURNS)
        return carry

    def first_product(j, total):
        index = 2 * chip(j)
        weighted = jnp.concatenate([w0buf[index], w0buf[index + 1]], axis=1)
        return total + product(weighted, table[j])

    def first_step(j, total):
        index = 2 * chip(j)
        wait_first(w0buf, w0rcv, index)
        wait_first(w0buf, w0rcv, index + 1)
        return first_product(j, total)

    wait_first(w0buf, w0rcv, 2 * q + other)
    lax.fori_loop(1, n, table_step, 0)
    field = first_product(jnp.int32(0), jnp.zeros((w0out.shape[1], 2 * LANES), jnp.float32))
    field = sums_of(first_step, field)

    def last_copy(z, x, s):
        block = wlast.at[c * n + q]
        return pltpu.make_async_remote_copy(
            block, block, lsend, lrcv.at[c * n + q], device_id=(g, z, x, s), device_id_type=MESH)

    def send_last(cores, i):
        z, x = near(n - 1 - i)
        for s in cores:
            last_copy(z, x, s).start()

    def update(r, total):
        fresh = state[...] - (total + inc[...]) * inv[...]
        weighted = (fresh * cell_area).astype(jnp.bfloat16)
        if r == ITERS - 1:
            wlast[c * n + q] = weighted
            each(0, n - 1, functools.partial(send_last, [0, 1]))
            last_copy(tz, sx, other).start()
            return fresh
        state[...] = fresh
        wbuf[r, q] = weighted

        def send(i):
            z, x = near(n - 1 - i)
            pltpu.make_async_remote_copy(
                wbuf.at[r, q], wbuf.at[r, q], wsend.at[r], wrcv.at[r % 2, q],
                device_id=(g, z, x, c), device_id_type=MESH).start()

        each(0, n - 1, send)
        return fresh

    def plane_step(j, carry):
        index = 2 * chip(j)
        build(plane.at[j], far_kernel, toward, index, 1.0)
        return carry

    def gathered(r):
        def step(j, sums):
            index = chip(j)
            slot = wbuf.at[r, index]
            pltpu.make_async_copy(slot, slot, wrcv.at[r % 2, index]).wait()
            return sums + product(wbuf[r, index], table[j])

        return sums_of(step, product(wbuf[r, q], table[0]))

    def last_wait(index):
        pltpu.make_async_copy(wlast.at[index], wlast.at[index], lrcv.at[index]).wait()

    def far_product(j):
        index = chip(j)
        return product(jnp.concatenate([wlast[index], wlast[n + index]], axis=0), plane[j])

    def far_step(j, sums):
        for s in range(2):
            last_wait(s * n + chip(j))
        return sums + far_product(j)

    share = -(-n // ITERS)
    for r in range(ITERS):
        fresh = update(r, field)
        last = r == ITERS - 1
        if last:
            low, high = fresh[:, :LANES], fresh[:, LANES:]
            swap_out[0] = jnp.where(c == 0, high, low)
            density_out[c] = jnp.where(c == 0, low, high)
            dswap = pltpu.make_async_remote_copy(
                swap_out.at[0], swap_in.at[0], xsend.at[3], xrcv.at[3],
                device_id=(g, tz, sx, other), device_id_type=MESH)
            dswap.start()
        lax.fori_loop(min(r * share, n), min((r + 1) * share, n), plane_step, 0)
        if last:
            dswap.wait_recv()
            density_out[other] = swap_in[0]
            continue
        field = gathered(r)

    def end_first(i):
        z, x = near(i)
        for s in range(2):
            for kind in range(2):
                first_copy(kind, z, x, s, 2 * i + s).wait_send()

    each(1, n, end_first)
    for kind in range(2):
        first_copy(kind, tz, sx, other, 0).wait_send()
    for r in range(ITERS - 1):
        sent = wbuf.at[r, pl.ds(0, n - 1)]
        pltpu.make_async_copy(sent, sent, wsend.at[r]).wait()
    for copy in swaps:
        copy.wait_send()
    dswap.wait_send()

    last_wait(other * n + q)
    far = sums_of(far_step, far_product(0))
    half = far_out.shape[1]
    far_out[0] = far[:half]
    far_out[1] = far[half:]

    sent = wlast.at[pl.ds(0, 2 * n - 1)]
    pltpu.make_async_copy(sent, sent, lsend).wait()


FOLD = np.polynomial.chebyshev.Chebyshev.interpolate(
    lambda v: -np.sin(2.0 * np.pi * np.sqrt(v)) / np.sqrt(v), 3, domain=[0.0, 0.0625]
).convert(kind=np.polynomial.Polynomial).coef
FOLD = [float(c) for c in FOLD]
MONIC = [c / FOLD[3] for c in FOLD[:3]]
KAPPA = (FOUR_PI / (FOLD[3] * TURNS)) ** 2
SOFT = (TURNS * SMOOTHING) ** 2
DEPTH = 32
ROWS = 64
DUE = (8, 8, 10)


def folded(turns):
    g = jnp.abs(turns - jnp.round(turns)) - 0.25
    return g, g * g


def parts_of(value):
    high = value.astype(jnp.bfloat16).astype(jnp.float32)
    rest = value - high
    middle = rest.astype(jnp.bfloat16).astype(jnp.float32)
    return high, middle, rest - middle


def stacked(groups):
    return jnp.concatenate(groups + [jnp.zeros_like(groups[0])] * (DEPTH // 4 - len(groups)), axis=0)


def column_kernel(sizes, cell_area, points, density, incident, precond, receivers, out,
                  xloc, dloc, iloc, ploc, rloc, pmsg, pbuf, dmsg, dbuf, left, right, aim, stage, table, plane,
                  state, inc, inv, wfin, wall, dsend, drcv,
                  lsem, psend, prcv, dsnd, drv, tsend, trcv, wsend, wrcv, osend, orcv):
    density_out, far_out = out.at[0], out.at[1]
    T, S = sizes
    n = T * S
    D = 2 * n
    wide = 2 * LANES
    share = dloc.shape[0] // D
    f32, bf16 = jnp.float32, jnp.bfloat16
    g, tz, sx, c = (lax.axis_index(a) for a in AXES)
    q = tz * S + sx
    me = 2 * q + c
    other = 1 - c

    def nearest(j):
        k, b = lax.div(j, S), lax.rem(j, S)
        inner = jnp.minimum(tz, T - 1 - tz)
        alternating = tz + lax.div(k + 1, 2) * (2 * lax.rem(k, 2) - 1)
        tail = jnp.where(tz <= T - 1 - tz, k, T - 1 - k)
        z = jnp.where(k <= 2 * inner, alternating, tail)
        x = lax.rem(sx + b, S)
        return z, x

    dests = [nearest(jnp.int32(j)) for j in range(n)]

    spots = []
    for k in range(n // 2):
        for h in (c, other):
            z, x = nearest(2 * k + h)
            spots.append(z * S + x)

    peers = [(dests[j], s) for j in range(1, n) for s in range(2)]
    sibling = (dests[0], other)

    def place(peer):
        (z, x), s = peer
        return (g, z, x, s)

    def index_of(peer):
        (z, x), s = peer
        return 2 * (z * S + x) + s

    loads = [
        pltpu.make_async_copy(points, xloc, lsem.at[0]),
        pltpu.make_async_copy(precond, ploc, lsem.at[1]),
        pltpu.make_async_copy(density, dloc, lsem.at[2]),
        pltpu.make_async_copy(incident, iloc, lsem.at[3]),
        pltpu.make_async_copy(receivers.at[me], rloc, lsem.at[4]),
    ]
    for load in loads:
        load.start()
    barrier = pltpu.get_barrier_semaphore()
    for peer in peers[::-1] + [sibling]:
        pl.semaphore_signal(barrier, inc=1, device_id=place(peer), device_id_type=MESH)
    for load in loads:
        load.wait()
    message = jnp.concatenate([xloc[...], 1.0 / ploc[...]], axis=0)
    pmsg[...] = message
    pbuf[me] = message
    for e in range(D):
        rows = slice(share * e, share * (e + 1))
        dmsg[e] = jnp.concatenate([dloc[rows, :], iloc[rows, :]], axis=0)
    dbuf[me] = dmsg[me]
    pl.semaphore_wait(barrier, D - 1)

    def send(source, target, send_sem, receive_sem, peer):
        pltpu.make_async_remote_copy(
            source, target, send_sem, receive_sem, device_id=place(peer), device_id_type=MESH).start()

    def await_in(target, semaphore):
        pltpu.make_async_copy(target, target, semaphore).wait()

    for peer in [sibling] + peers[::-1]:
        send(pmsg, pbuf.at[me], psend, prcv.at[tz], peer)
    for peer in [sibling] + peers:
        send(dmsg.at[index_of(peer)], dbuf.at[me], dsnd, drv, peer)

    row4 = lax.broadcasted_iota(jnp.int32, (4, wide), 0)
    coordinate = row4 < 3

    def product(a, b):
        return lax.dot_general(a, b, (((1,), (0,)), ((), ())), preferred_element_type=f32)

    def features(p):
        index = 2 * spots[p]
        x = jnp.concatenate([pbuf[index], pbuf[index + 1]], axis=1) * TURNS
        squares = x * x
        a = squares[0:1] + squares[1:2] + squares[2:3]
        high, middle, low = parts_of(jnp.where(coordinate, x, a))
        scale = jnp.where(coordinate, -2.0, 1.0)
        high, middle, low = high * scale, middle * scale, low * scale
        ones = jnp.where(coordinate, 1.0, 0.0)
        left[p] = stacked([high, high, high, middle, middle, low, ones]).T.astype(bf16)
        for h, (factor, shift) in enumerate(((1.0, 0.0), (KAPPA, KAPPA * SOFT))):
            high, middle, low = parts_of(jnp.where(coordinate, x, 1.0) * factor)
            tail = jnp.concatenate(list(parts_of(a * factor + shift)) + [jnp.zeros_like(a)], axis=0)
            right[p, :, h * wide:(h + 1) * wide] = stacked(
                [high, middle, low, high, middle, high, tail]).astype(bf16)

    def entries(pair, diagonal):
        squared, softened = pair[:, :wide], pair[:, wide:]
        if diagonal is not None:
            squared = jnp.where(diagonal, 0.0, squared)
            softened = jnp.where(diagonal, KAPPA * SOFT, softened)
        turns = squared * lax.rsqrt(jnp.maximum(squared, 1e-30))
        fold, v = folded(turns)
        total = ((v + MONIC[2]) * v + MONIC[1]) * v + MONIC[0]
        return (total * fold * lax.rsqrt(softened)).astype(bf16)

    def distances(unit, slot):
        for i, (a, b) in enumerate(unit):
            stage[slot, i] = product(left[a], right[b])

    def shade(unit, slot):
        for start in range(0, wide, ROWS):
            rows = slice(start, start + ROWS)
            for i, (a, b) in enumerate(unit):
                diagonal = None
                if a == b:
                    shape = (ROWS, wide)
                    diagonal = lax.broadcasted_iota(jnp.int32, shape, 0) + start == lax.broadcasted_iota(jnp.int32, shape, 1)
                table[a, b, rows, :] = entries(stage[slot, i, rows, :], diagonal)

    def swap(k, b):
        return pltpu.make_async_remote_copy(
            table.at[2 * k, b], table.at[2 * k + 1, b ^ 1], tsend.at[k], trcv.at[k],
            device_id=place(sibling), device_id_type=MESH)

    def flip(a, b):
        table[b, a] = table[a, b].T

    def swapped(k):
        return table.at[0, pl.ds(0, 2 * k + 1)]

    rows3 = directions(rloc[...])
    aims = jnp.concatenate(list(rows3) + [jnp.zeros_like(rows3[0])], axis=0) * -0.5
    high, middle, low = parts_of(aims)
    aim[...] = stacked([high, middle, low, high, middle, high]).astype(bf16)

    def plane_in(k):
        count = 4 if k else 3
        await_in(pbuf.at[pl.ds(0, count)], prcv.at[dests[2 * k][0]])
        features(2 * k)
        features(2 * k + 1)

    def columns_in():
        await_in(dbuf.at[pl.ds(0, D - 1)], drv)
        state[...] = jnp.zeros_like(state)
        inc[...] = jnp.zeros_like(inc)
        inv[...] = jnp.zeros_like(inv)
        for p in range(n):
            for s in range(2):
                index = 2 * spots[p] + s
                lanes = slice((2 * p + s) * LANES, (2 * p + s + 1) * LANES)
                message = dbuf[index]
                state[0:share, lanes] = message[:share]
                inc[0:share, lanes] = message[share:]
                inv[0:share, lanes] = jnp.broadcast_to(pbuf[index][3:4], (share, LANES))

    units = []
    for k in range(n // 2):
        units += [(k, [(2 * k, 2 * m), (2 * k, 2 * m + 1)]) for m in range(k)]
        units += [(k, [(2 * k, 2 * k), (2 * k + 1, 2 * k)])]
    last = n // 2 - 1
    plane_in(0)
    distances(units[0][1], 0)
    flips = []
    for i, (k, unit) in enumerate(units):
        following = units[i + 1] if i + 1 < len(units) else None
        if following and following[0] != k:
            plane_in(following[0])
        for old in range(last):
            if i == DUE[old]:
                await_in(swapped(old), trcv.at[old])
                flips += [(2 * old + 1, b) for b in range(2 * old)]
        for a, b in flips:
            flip(a, b)
        if following:
            distances(following[1], (i + 1) % 2)
        shade(unit, i % 2)
        flips = [(a, b) for a, b in unit if a != b]
        for a, b in unit:
            if a == 2 * k:
                swap(k, b).start()
        if i == len(units) - 2:
            columns_in()
    for old in range(last):
        if DUE[old] >= len(units):
            await_in(swapped(old), trcv.at[old])
            flips += [(2 * old + 1, b) for b in range(2 * old)]
    for a, b in flips:
        flip(a, b)

    def piece(value, p):
        return value[:, p * wide:(p + 1) * wide]

    def gather_field(weighted, sources, b):
        total = None
        for a in sources:
            part = product(piece(weighted, a), table[a, b])
            total = part if total is None else total + part
        return total

    def update(field, b):
        lanes = slice(b * wide, (b + 1) * wide)
        state[:, lanes] = state[:, lanes] - (field + inc[:, lanes]) * inv[:, lanes]

    weighted = (state[...] * cell_area).astype(bf16)
    fields = [gather_field(weighted, range(n - 1), b) for b in range(n - 1)]
    await_in(swapped(last), trcv.at[last])
    for b in range(n - 2):
        flip(n - 1, b)
    for b in range(n - 1):
        update(fields[b] + product(piece(weighted, n - 1), table[n - 1, b]), b)
    update(gather_field(weighted, range(n), n - 1), n - 1)

    def iterate(r, carry):
        weighted = (state[...] * cell_area).astype(bf16)
        for b in range(n):
            update(gather_field(weighted, range(n), b), b)
        return carry

    lax.fori_loop(1, ITERS - 1, iterate, 0)

    def final_copy(k, peer):
        block = pl.ds(S * dests[2 * k][0], S)
        return pltpu.make_async_remote_copy(
            wfin.at[block], wall.at[me, block], wsend, wrcv, device_id=place(peer), device_id_type=MESH)

    weighted = (state[...] * cell_area).astype(bf16)
    for k in range(n // 2):
        for p in (2 * k, 2 * k + 1):
            update(gather_field(weighted, range(n), p), p)
            wfin[spots[p]] = (state[0:share, p * wide:(p + 1) * wide] * cell_area).astype(bf16)
        for peer in peers[::-1] + [sibling]:
            final_copy(k, peer).start()
    for p in range(n):
        for s in range(2):
            dsend[2 * spots[p] + s] = state[0:share, (2 * p + s) * LANES:(2 * p + s + 1) * LANES]
    for peer in peers[::-1] + [sibling]:
        send(dsend.at[index_of(peer)], drcv.at[me], osend, orcv, peer)
    wall[me] = wfin[...]
    drcv[me] = dsend[me]

    def plane_step(j, carry):
        fold, v = folded(product(left[j], aim[...]))
        total = ((FOLD[3] * v + FOLD[2]) * v + FOLD[1]) * v + FOLD[0]
        plane[j] = (total * fold).astype(bf16)
        return carry

    lax.fori_loop(0, n, plane_step, 0)

    def finish_sends():
        for k in range(n // 2):
            await_in(swapped(k), tsend.at[k])
        await_in(pbuf.at[pl.ds(0, D - 1)], psend)
        await_in(dbuf.at[pl.ds(0, D - 1)], dsnd)

    finish_sends()
    await_in(wall.at[pl.ds(0, D - 1)], wrcv)
    for j in range(n):
        index = spots[j]
        gathered = jnp.concatenate([wall[d, index].astype(f32) for d in range(D)], axis=0).astype(bf16)
        part = product(gathered, plane[j])
        far = part if j == 0 else far + part
    half = far_out.shape[1]
    far_out[0] = far[:half]
    far_out[1] = far[half:]
    await_in(drcv.at[pl.ds(0, D - 1)], orcv)
    whole = jnp.concatenate([drcv[d] for d in range(D)], axis=0)
    density_out[0] = whole[:half]
    density_out[1] = whole[half:]
    await_in(wall.at[pl.ds(0, D - 1)], wsend)
    await_in(drcv.at[pl.ds(0, D - 1)], osend)


def column_call(sizes, cell_area, points, density, incident, precond, receivers):
    T, S = sizes
    n = T * S
    D = 2 * n
    columns, own = density.shape
    half = columns // 2
    share = columns // D
    wide = 2 * own
    f32, bf16 = jnp.float32, jnp.bfloat16
    anywhere = pl.BlockSpec(memory_space=pl.ANY)
    dma = pltpu.SemaphoreType.DMA
    return pl.pallas_call(
        functools.partial(column_kernel, sizes, cell_area),
        out_shape=jax.ShapeDtypeStruct((2, 2, half, own), f32),
        in_specs=[anywhere] * 5,
        out_specs=pl.BlockSpec(memory_space=pltpu.VMEM),
        scratch_shapes=[
            pltpu.VMEM((3, own), f32),
            pltpu.VMEM((columns, own), f32),
            pltpu.VMEM((columns, own), f32),
            pltpu.VMEM((1, own), f32),
            pltpu.VMEM((1, own), jnp.int32),
            pltpu.VMEM((4, own), f32),
            pltpu.VMEM((D, 4, own), f32),
            pltpu.VMEM((D, 2 * share, own), f32),
            pltpu.VMEM((D, 2 * share, own), f32),
            pltpu.VMEM((n, wide, DEPTH), bf16),
            pltpu.VMEM((n, DEPTH, 2 * wide), bf16),
            pltpu.VMEM((DEPTH, own), bf16),
            pltpu.VMEM((2, 2, wide, 2 * wide), f32),
            pltpu.VMEM((n, n, wide, wide), bf16),
            pltpu.VMEM((n, wide, own), bf16),
            pltpu.VMEM((8, n * wide), f32),
            pltpu.VMEM((8, n * wide), f32),
            pltpu.VMEM((8, n * wide), f32),
            pltpu.VMEM((n, share, wide), bf16),
            pltpu.VMEM((D, n, share, wide), bf16),
            pltpu.VMEM((D, share, own), f32),
            pltpu.VMEM((D, share, own), f32),
            dma((5,)),
            dma(()),
            dma((T,)),
            dma(()),
            dma(()),
            dma((n // 2,)),
            dma((n // 2,)),
            dma(()),
            dma(()),
            dma(()),
            dma(()),
        ],
        compiler_params=pltpu.CompilerParams(
            collective_id=0, has_side_effects=True, vmem_limit_bytes=60 * 1024 * 1024),
    )(
        points, density, incident, precond.reshape(1, own), receivers.reshape(D, 1, own),
    )


def shards(points, density, incident, precond, receivers):
    T, S = lax.axis_size("tgt"), lax.axis_size("src")
    n = T * S
    columns, own = density.shape
    half = columns // 2
    f32, bf16 = jnp.float32, jnp.bfloat16
    cell_area = FOUR_PI / (own * n * 2)
    if S == 2 and n <= 8 and columns == 4 * n and own == LANES:
        out = column_call((T, S), cell_area, points, density, incident, precond, receivers)
        return out[0].reshape(columns, own), out[1].reshape(columns, own)
    block = pltpu.VMEM((2, 2, half, own), f32)
    anywhere = pl.BlockSpec(memory_space=pl.ANY)
    vmem = pl.BlockSpec(memory_space=pltpu.VMEM)
    dma = pltpu.SemaphoreType.DMA
    out = pl.pallas_call(
        functools.partial(kernel, (T, S), cell_area),
        out_shape=block,
        in_specs=[anywhere] * 5,
        out_specs=vmem,
        scratch_shapes=[
            pltpu.VMEM((2 * n, 3, own), f32),
            pltpu.VMEM((2 * n, half, own), bf16),
            pltpu.VMEM((ITERS - 1, n, half, 2 * own), bf16),
            pltpu.VMEM((2 * n, half, 2 * own), bf16),
            pltpu.VMEM((n, 2 * own, 2 * own), bf16),
            pltpu.VMEM((n, own, 2 * own), bf16),
            pltpu.VMEM((3, 2 * own, own), f32),
            pltpu.VMEM((3, own, own), f32),
            pltpu.VMEM((2, half, own), bf16),
            pltpu.VMEM((2, half, own), f32),
            pltpu.VMEM((2, half, own), f32),
            pltpu.VMEM((1, own), f32),
            pltpu.VMEM((1, own), jnp.int32),
            pltpu.VMEM((half, own), f32),
            pltpu.VMEM((half, own), f32),
            pltpu.VMEM((1, own), f32),
            pltpu.VMEM((half, 2 * own), f32),
            pltpu.VMEM((half, 2 * own), f32),
            pltpu.VMEM((1, 2 * own), f32),
            pltpu.VMEM((1, half, own), f32),
            pltpu.VMEM((1, half, own), f32),
            dma((5,)),
            dma((2 * n,)),
            dma((2 * n,)),
            dma((ITERS - 1,)),
            dma(()),
            dma((2 * n,)),
            dma((2 * n,)),
            dma((2, n)),
            dma((2 * n,)),
            dma((4,)),
            dma((4,)),
        ],
        compiler_params=pltpu.CompilerParams(
            collective_id=0, has_side_effects=True, vmem_limit_bytes=60 * 1024 * 1024),
    )(
        points,
        density.reshape(2, half, own),
        incident.reshape(2, half, own),
        precond.reshape(1, own),
        receivers.reshape(2 * n, 1, own),
    )
    return out[0].reshape(columns, own), out[1].reshape(columns, own)


def solution(mesh):
    split = P(None, AXES)
    return jax.shard_map(
        shards,
        mesh=mesh,
        in_specs=(split, split, split, P(AXES), P("groups")),
        out_specs=(split, split),
        check_vma=False,
    )
```
